32 devices in a mesh: blk: 8 (over z, x), grp: 4 (over y, core).
Axes of the slice: x: 2, y: 2, z: 4, core: 2. Of those that a mesh axis runs over, the one named last changes fastest.
Arguments:
- queries: bfloat16 [16384, 512], P(('blk', 'grp')), may hold values from -64 to 64
- keys: bfloat16 [16384, 128], P(('blk', 'grp')), may hold values from -8 to 8
- values: bfloat16 [16384, 128], P(('blk', 'grp')), may hold values from -6 to 6
- selected: int32 [32, 16], replicated, may hold values from 0 to 255, as said below
- key_in: bfloat16 [4096, 256], replicated, may hold values from -0.09375 to 0.09375
- key_out: bfloat16 [256, 128], replicated, may hold values from -0.375 to 0.375
- value_in: bfloat16 [4096, 256], replicated, may hold values from -0.09375 to 0.09375
- value_out: bfloat16 [256, 128], replicated, may hold values from -0.375 to 0.375
- positions: bfloat16 [2, 32, 128], replicated, may hold values from -5 to 5
- gate_weight: bfloat16 [512, 12], replicated, may hold values from -0.25 to 0.25
Outputs:
- attended: bfloat16 [16384, 512], P(('blk', 'grp'))
The draws below stay inside these ranges and needn't reach their ends.
Inputs may be any that keep to these rules, and one draw needn't show every extreme that they name: `selected`: row d lists 16 different fine blocks. Write r = 32 and b = d // 4. Entry 0 is the first fine block of group d's own tokens. Every listed block j with j // r different from b has j // r < b, and no two listed blocks share a value of j // r other than b. Blocks with j // r == b may lie after group d's tokens.
All inputs are finite; a program needn't handle non-finite values.
Results may differ from the reference program's by a relative error of at most 0.004.
Values may be sent and summed in bfloat16 or wider, within the bound.
A program may use at most 64 MiB of HBM per device.

```python
import jax
import jax.numpy as jnp
from jax import lax

HEAD_DIM = 128
HEADS = 4
CMP_HIDDEN = 256
CMP_BLOCK = 32
SEL_BLOCK = 64
TOPN = 16
WINDOW = 512
TOK_DEV = 512
SEQ = 16384
NCMP = 512
GROUPS = 32
N_BLK = 8
N_GRP = 4


def keys_law(key):
    base_key = jax.random.fold_in(key, 11)
    second_key = jax.random.fold_in(base_key, 1)
    return jnp.clip(jax.random.normal(second_key, (SEQ, HEAD_DIM), jnp.float32), -6.0, 6.0)


def draw_keys(key, part):
    return keys_law(key).astype(jnp.bfloat16)


def draw_queries(key, part):
    own_key = jax.random.fold_in(key, 5)
    base = jnp.clip(jax.random.normal(own_key, (SEQ, HEADS * HEAD_DIM), jnp.float32), -6.0, 6.0)
    return base.astype(jnp.bfloat16)


def draw_selected(key, part):
    groups = N_BLK * N_GRP
    per_row = N_GRP * TOK_DEV // SEL_BLOCK
    base_key = jax.random.fold_in(key, 23)
    key_rows, key_blocks, key_own = jax.random.split(base_key, 3)
    group_ids = jnp.arange(groups, dtype=jnp.int32)
    group_row = group_ids // N_GRP
    group_col = group_ids % N_GRP
    row_ids = jnp.arange(N_BLK, dtype=jnp.int32)
    row_score = jax.random.randint(key_rows, (groups, N_BLK), 1, 1 << 20) * N_BLK + row_ids[None, :]
    row_score = jnp.where(row_ids[None, :] == 0, 1 << 28, row_score)
    eligible = row_ids[None, :] < group_row[:, None]
    row_score = jnp.where(eligible, row_score, -1)
    rank = jnp.sum((row_score[:, None, :] > row_score[:, :, None]).astype(jnp.int32), axis=2)
    chosen = eligible & (rank < TOPN - 1)
    remote_count = jnp.sum(chosen.astype(jnp.int32), axis=1)
    slots = jnp.arange(TOPN - 1, dtype=jnp.int32)
    hit = chosen[:, None, :] & (rank[:, None, :] == slots[None, :, None])
    row_of_slot = jnp.sum(jnp.where(hit, row_ids[None, None, :], 0), axis=2)
    remote_blocks = row_of_slot * per_row + jax.random.randint(key_blocks, (groups, TOPN - 1), 0, per_row)
    first_local = group_col * (TOK_DEV // SEL_BLOCK)
    local_ids = jnp.arange(per_row, dtype=jnp.int32)
    own_score = jax.random.randint(key_own, (groups, per_row), 0, 1 << 20) * per_row + local_ids[None, :]
    own_score = jnp.where(local_ids[None, :] == first_local[:, None], -1, own_score)
    best_scores, unused = jax.lax.top_k(own_score, TOPN - 1)
    own_extra = group_row[:, None] * per_row + best_scores % per_row
    own_index = jnp.clip(slots[None, :] - remote_count[:, None], 0, TOPN - 2)
    own_pick = jnp.take_along_axis(own_extra, own_index, axis=1)
    tail = jnp.where(slots[None, :] < remote_count[:, None], remote_blocks, own_pick)
    head = (group_row * per_row + first_local)[:, None]
    return jnp.concatenate([head, tail], axis=1).astype(jnp.int32)


def level_of(key, extent, cuts, low, high):
    def one(axis_at, shards_of):
        heights = jax.random.uniform(jax.random.fold_in(jax.random.fold_in(key, 6), axis_at), (shards_of,), jnp.float32, low / len(cuts), high / len(cuts))
        return jnp.repeat(jnp.exp(heights), extent[axis_at] // shards_of).reshape((-1,) + (1,) * (len(extent) - axis_at - 1))

    level = one(*cuts[0])
    for cut in cuts[1:]:
        level = level * one(*cut)
    return level


def centred(rng, shape, deviation, limit, cuts=(), kind=jnp.bfloat16):
    values = jax.random.normal(rng, shape, jnp.float32) * deviation
    if len(cuts) > 0:
        values = level_of(rng, shape, cuts, -0.22, 0.18) * values
    return jnp.clip(values, min=-limit, max=limit).astype(kind)


def setup_inputs(seed: int = 0) -> dict:
    streams_of = jax.random.split(jax.random.key(seed), 11)
    queries = draw_queries(jax.random.fold_in(streams_of[10], 71), 0)
    keys = draw_keys(jax.random.fold_in(streams_of[10], 71), 0)
    values = centred(streams_of[2], (SEQ, HEAD_DIM), 1.0, 6.0, ((0, 32),))
    selected = draw_selected(jax.random.fold_in(streams_of[10], 71), 0)
    key_in = centred(streams_of[4], (CMP_BLOCK * HEAD_DIM, CMP_HIDDEN), (CMP_BLOCK * HEAD_DIM) ** -0.5, 0.09375)
    key_out = centred(streams_of[5], (CMP_HIDDEN, HEAD_DIM), CMP_HIDDEN ** -0.5, 0.375)
    value_in = centred(streams_of[6], (CMP_BLOCK * HEAD_DIM, CMP_HIDDEN), (CMP_BLOCK * HEAD_DIM) ** -0.5, 0.09375)
    value_out = centred(streams_of[7], (CMP_HIDDEN, HEAD_DIM), CMP_HIDDEN ** -0.5, 0.375)
    positions = centred(streams_of[8], (2, CMP_BLOCK, HEAD_DIM), 1.0, 5.0)
    gate_weight = centred(streams_of[9], (HEADS * HEAD_DIM, 3 * HEADS), (HEADS * HEAD_DIM) ** -0.5, 0.25)
    return dict(queries=queries, keys=keys, values=values, selected=selected, key_in=key_in, key_out=key_out, value_in=value_in, value_out=value_out, positions=positions, gate_weight=gate_weight)


NEG = -1e30


def compress(tokens, shift, w_in, w_out):
    count = tokens.shape[0] // CMP_BLOCK
    mixed = tokens.astype(jnp.float32).reshape(count, CMP_BLOCK, HEAD_DIM) + shift.astype(jnp.float32)[None]
    flat = mixed.astype(jnp.bfloat16).reshape(count, CMP_BLOCK * HEAD_DIM)
    hidden = jax.nn.silu(jnp.dot(flat, w_in, preferred_element_type=jnp.float32)).astype(jnp.bfloat16)
    return jnp.dot(hidden, w_out, preferred_element_type=jnp.float32).astype(jnp.bfloat16)


def attend(query_rows, query_pos, key_rows, value_rows, key_pos, span):
    scale = HEAD_DIM ** -0.5
    scores = jnp.einsum("qhd,kd->qhk", query_rows.astype(jnp.float32), key_rows.astype(jnp.float32)) * scale
    allowed = (key_pos[None, :] <= query_pos[:, None]) & (key_pos[None, :] > query_pos[:, None] - span) & (key_pos[None, :] >= 0)
    scores = jnp.where(allowed[:, None, :], scores, NEG)
    top = jnp.max(scores, axis=2, keepdims=True)
    weights = jnp.exp(scores - top)
    total = jnp.sum(weights, axis=2)
    mixed = jnp.einsum("qhk,kd->qhd", weights.astype(jnp.bfloat16).astype(jnp.float32), value_rows.astype(jnp.float32))
    return mixed / total[..., None]


def reference(queries, keys, values, selected, key_in, key_out, value_in, value_out, positions, gate_weight):
    scale = HEAD_DIM ** -0.5
    comp_keys = compress(keys, positions[0], key_in, key_out)
    comp_values = compress(values, positions[1], value_in, value_out)
    comp_end = jnp.arange(NCMP, dtype=jnp.int32) * CMP_BLOCK + (CMP_BLOCK - 1)
    padded_keys = jnp.concatenate([jnp.zeros((WINDOW, HEAD_DIM), keys.dtype), keys], axis=0)
    padded_values = jnp.concatenate([jnp.zeros((WINDOW, HEAD_DIM), values.dtype), values], axis=0)

    def group(index):
        first = index * TOK_DEV
        flat_rows = lax.dynamic_slice_in_dim(queries, first, TOK_DEV, 0)
        rows = flat_rows.reshape(TOK_DEV, HEADS, HEAD_DIM)
        query_pos = first + jnp.arange(TOK_DEV, dtype=jnp.int32)
        scores = jnp.einsum("qhd,kd->qhk", rows.astype(jnp.float32), comp_keys.astype(jnp.float32)) * scale
        seen = comp_end[None, :] <= query_pos[:, None]
        scores = jnp.where(seen[:, None, :], scores, NEG)
        top = jnp.maximum(jnp.max(scores, axis=2, keepdims=True), 0.0)
        weights = jnp.exp(scores - top)
        total = jnp.exp(-top[..., 0]) + jnp.sum(weights, axis=2)
        coarse = jnp.einsum("qhk,kd->qhd", weights.astype(jnp.bfloat16).astype(jnp.float32), comp_values.astype(jnp.float32)) / total[..., None]
        chosen = lax.dynamic_index_in_dim(selected, index, 0, keepdims=False)
        token_ids = (chosen[:, None] * SEL_BLOCK + jnp.arange(SEL_BLOCK, dtype=jnp.int32)[None, :]).reshape(-1)
        fine = attend(rows, query_pos, jnp.take(keys, token_ids, axis=0), jnp.take(values, token_ids, axis=0), token_ids, SEQ + 1)
        window_keys = lax.dynamic_slice_in_dim(padded_keys, first, TOK_DEV + WINDOW, 0)
        window_values = lax.dynamic_slice_in_dim(padded_values, first, TOK_DEV + WINDOW, 0)
        window_pos = first - WINDOW + jnp.arange(TOK_DEV + WINDOW, dtype=jnp.int32)
        local = attend(rows, query_pos, window_keys, window_values, window_pos, WINDOW)
        gates = jax.nn.sigmoid(jnp.dot(flat_rows, gate_weight, preferred_element_type=jnp.float32)).reshape(TOK_DEV, 3, HEADS)
        mixed = gates[:, 0, :, None] * coarse + gates[:, 1, :, None] * fine + gates[:, 2, :, None] * local
        return mixed.astype(jnp.bfloat16).reshape(TOK_DEV, HEADS * HEAD_DIM)

    result = lax.map(group, jnp.arange(GROUPS, dtype=jnp.int32))
    return result.reshape(SEQ, HEADS * HEAD_DIM)
```

```python
import functools
import math

import jax
import jax.numpy as jnp
from jax import lax
from jax.experimental import pallas as pl
from jax.experimental.pallas import tpu as pltpu
from jax.sharding import PartitionSpec as P

HEAD_DIM = 128
HEADS = 4
CMP_BLOCK = 32
SEL_BLOCK = 64
TOPN = 16
WINDOW = 512
ROWS = 128

NEG = -1e30
RATE = HEAD_DIM**-0.5 * math.log2(math.e)
MESH = pl.DeviceIdType.MESH
F32 = jnp.float32
BF16 = jnp.bfloat16


def across(a, b):
    return lax.dot_general(a, b, (((1,), (1,)), ((), ())), preferred_element_type=F32)


def branch(parts, value_parts, floor):
    top = functools.reduce(jnp.maximum, [jnp.max(s, axis=0, keepdims=True) for s in parts])
    total = 0.0
    if floor:
        top = jnp.maximum(top, 0.0)
        total = jnp.exp2(-top * RATE)
    mixed = 0.0
    for s, v in zip(parts, value_parts):
        weights = jnp.exp2((s - top) * RATE)
        total = total + jnp.sum(weights, axis=0, keepdims=True)
        mixed = mixed + jnp.dot(v, weights.astype(BF16), preferred_element_type=F32)
    return mixed, total


def kernel(
    B,
    G,
    sel,
    queries,
    keys,
    values,
    key_in,
    key_out,
    value_in,
    value_out,
    positions,
    gate_weight,
    out,
    w_in,
    w_out,
    shifted,
    sk,
    sv,
    pk,
    pv,
    ik,
    iv,
    stk,
    stv,
    cc,
    cvt,
    wk,
    wvt,
    fk,
    fv,
    fvt,
    pool,
    acc,
    gates,
    w_sem,
    a_s,
    a_r,
    m_s,
    m_r,
    p_s,
    p_r,
    b_s,
    b_r,
    c_s,
    c_r,
    f_s,
    f_r,
):
    T = keys.shape[0] * SEL_BLOCK
    N = T // CMP_BLOCK
    Y = G // 2
    per_row = G * T // SEL_BLOCK
    b = lax.axis_index("blk")
    g = lax.axis_index("grp")
    y = g // 2
    core = g % 2
    mate = g + 1 - 2 * core
    position = b * G + g
    first = position * T

    loads = [
        pltpu.make_async_copy(src, dst, w_sem.at[n])
        for n, (src, dst) in enumerate(
            (
                (key_in, w_in.at[0]),
                (value_in, w_in.at[1]),
                (key_out, w_out.at[0]),
                (value_out, w_out.at[1]),
            )
        )
    ]
    for load in loads:
        load.start()

    cc[...] = jnp.zeros_like(cc)
    pk[...] = jnp.zeros_like(pk)
    pv[...] = jnp.zeros_like(pv)

    def remote(src, dst, send, recv, dev):
        return pltpu.make_async_remote_copy(
            src_ref=src,
            dst_ref=dst,
            send_sem=send,
            recv_sem=recv,
            device_id=dev,
            device_id_type=MESH,
        )

    def at(stretch, column):
        return {"blk": stretch, "grp": column}

    last = jnp.logical_and(g == G - 1, b < B - 1)
    head = jnp.logical_and(g == 0, b > 0)
    barrier = pltpu.get_barrier_semaphore()

    def greet(dev):
        pl.semaphore_signal(barrier, inc=1, device_id=dev, device_id_type=MESH)

    for e in range(1, G):
        greet(at(b, (g + e) % G))
    for d in range(1, B):
        greet(at((b + d) % B, g))

    @pl.when(last)
    def _():
        greet(at(b + 1, 0))

    @pl.when(head)
    def _():
        greet(at(b - 1, G - 1))

    here = pl.ds(g * (T // SEL_BLOCK), T // SEL_BLOCK)
    sk[here] = keys[...]
    sv[here] = values[...]
    pl.semaphore_wait(barrier, G - 1 + B - 1 + last.astype(jnp.int32) + head.astype(jnp.int32))

    own = (keys, values)
    row = (sk, sv)
    prev = (pk, pv)
    staged = (stk, stv)
    inbox = (ik, iv)

    def slot(column):
        return pl.ds(column * (T // SEL_BLOCK), T // SEL_BLOCK)

    def over_y(c, e):
        return remote(
            own[c], row[c].at[slot(g)], a_s.at[c, e], a_r.at[c, e], at(b, ((y + e) % Y) * 2 + core)
        )

    def to_mate(c, e):
        source = ((y - e + Y) % Y) * 2 + core
        src = own[c] if e == 0 else row[c].at[slot(source)]
        return remote(src, row[c].at[slot(source)], m_s.at[c, e], m_r.at[c, e], at(b, mate))

    def to_next(c):
        return remote(own[c], prev[c], p_s.at[c], p_r.at[c], at((b + 1) % B, 0))

    def block_out(c, d):
        return remote(
            staged[c].at[d - 1], inbox[c].at[b], b_s.at[c, d], b_r.at[c, d], at((b + d) % B, g)
        )

    def coarse_out(d):
        part = cc.at[g, :, pl.ds(pl.multiple_of(b * N, N), N), :]
        return remote(part, part, c_s.at[d], c_r.at[d], at((b + d) % B, g))

    def coarse_share(e):
        return remote(cc.at[g], cc.at[g], f_s.at[e], f_r.at[e], at(b, (g + e) % G))

    for c in range(2):
        for e in range(1, Y):
            over_y(c, e).start()
        to_mate(c, 0).start()

        @pl.when(last)
        def _(c=c):
            to_next(c).start()

    for c in range(2):
        shift = positions[c].astype(F32)
        shifted[c] = (
            own[c][...].astype(F32).reshape(N, CMP_BLOCK, HEAD_DIM) + shift[None]
        ).reshape(T, HEAD_DIM)
    for load in loads:
        load.wait()
    mine_rows = pl.ds(pl.multiple_of(b * N, N), N)
    for c in range(2):
        flat = jnp.concatenate(
            [shifted[c, pl.ds(t, N, stride=CMP_BLOCK), :].astype(BF16) for t in range(CMP_BLOCK)],
            axis=1,
        )
        hidden = jax.nn.silu(jnp.dot(flat, w_in[c], preferred_element_type=F32)).astype(BF16)
        cc[g, c, mine_rows, :] = jnp.dot(hidden, w_out[c], preferred_element_type=F32).astype(BF16)
    for d in range(1, B):

        @pl.when(b + d < B)
        def _(d=d):
            coarse_out(d).start()

    def home(j):
        owner = lax.div(j, per_row)
        return owner, j - owner * per_row

    def same(left, right):
        gap = left - right
        return 1 - jnp.minimum(jnp.maximum(gap, -gap), 1)

    picks = []
    for d in range(1, B):
        line = jnp.minimum(b + d, B - 1) * G + g
        pick = jnp.int32(0)
        for i in range(TOPN):
            owner, rank = home(sel[line, i])
            pick = pick + same(owner, b) * rank
        picks.append(pick)

    gates[...] = jax.nn.sigmoid(
        lax.dot_general(
            gate_weight[...], queries[...], (((0,), (1,)), ((), ())), preferred_element_type=F32
        )
    )

    for c in range(2):
        for e in range(1, Y):
            over_y(c, e).wait_recv()
            to_mate(c, e).start()
        for e in range(Y):
            to_mate(c, e).wait_recv()
        for d in range(1, B):

            @pl.when(b + d < B)
            def _(c=c, d=d):
                staged[c][d - 1] = row[c][picks[d - 1]]

        for d in range(1, B):

            @pl.when(b + d < B)
            def _(c=c, d=d):
                block_out(c, d).start()

    for d in range(1, B):

        @pl.when(b - d >= 0)
        def _(d=d):
            coarse_out(d).wait_recv()

    for e in range(1, G):
        coarse_share(e).start()

    @pl.when(head)
    def _():
        for c in range(2):
            to_next(c).wait_recv()

    before = slot(jnp.maximum(g - 1, 0))
    flat = (T, HEAD_DIM)
    wk[pl.ds(0, T), :] = jnp.where(g == 0, pk[...], sk[before]).reshape(flat)
    wk[pl.ds(T, T), :] = keys[...].reshape(flat)
    wvt[:, pl.ds(0, T)] = jnp.where(g == 0, pv[...], sv[before]).reshape(flat).T
    wvt[:, pl.ds(T, T)] = values[...].reshape(flat).T

    lanes = HEADS * ROWS

    def query_block(start):
        rows = queries[pl.ds(start, ROWS), :]
        return jnp.concatenate(
            [rows[:, h * HEAD_DIM : (h + 1) * HEAD_DIM] for h in range(HEADS)], axis=0
        )

    def gate(n, start):
        return jnp.concatenate(
            [gates[n * HEADS + h : n * HEADS + h + 1, pl.ds(start, ROWS)] for h in range(HEADS)],
            axis=1,
        )

    def iotas(count):
        k = lax.broadcasted_iota(jnp.int32, (count, lanes), 0)
        q = lax.broadcasted_iota(jnp.int32, (count, lanes), 1) % ROWS
        return k, q

    def window_step(step, carry):
        start = pl.multiple_of(step * ROWS, ROWS)
        span = pl.ds(pl.multiple_of(start + T - WINDOW, ROWS), ROWS + WINDOW)
        s = across(wk[span, :], query_block(start))
        k, q = iotas(ROWS)
        opening = jnp.where(position == 0, WINDOW - start, 0)
        kk = lax.broadcasted_iota(jnp.int32, (WINDOW - ROWS, lanes), 0) + ROWS
        parts = [
            jnp.where((k > q) & (k >= opening), s[:ROWS], NEG),
            jnp.where(kk >= opening, s[ROWS:WINDOW], NEG),
            jnp.where(k <= q, s[WINDOW:], NEG),
        ]
        vt = wvt[:, span]
        mixed, total = branch(parts, [vt[:, :ROWS], vt[:, ROWS:WINDOW], vt[:, WINDOW:]], False)
        acc[step] = mixed * (gate(2, start) / total)
        return carry

    lax.fori_loop(0, T // ROWS, window_step, 0)

    for e in range(1, G):
        coarse_share(e).wait_recv()
    for column in range(G):
        cvt[:, pl.ds(column * B * N, B * N)] = cc[column, 1].T

    def coarse_step(step, carry):
        start = pl.multiple_of(step * ROWS, ROWS)
        query = query_block(start)
        k, q = iotas(B * N)
        end = (k // N) * (G * T) + (k % N) * CMP_BLOCK + CMP_BLOCK - 1 - q
        parts = []
        for column in range(G):
            s = across(cc[column, 0], query)
            parts.append(jnp.where(end <= first + start - column * T, s, NEG))
        vts = [cvt[:, pl.ds(column * B * N, B * N)] for column in range(G)]
        mixed, total = branch(parts, vts, True)
        acc[step] = acc[step] + mixed * (gate(0, start) / total)
        return carry

    lax.fori_loop(0, T // ROWS, coarse_step, 0)

    for c in range(2):
        for d in range(1, B):

            @pl.when(b - d >= 0)
            def _(c=c, d=d):
                block_out(c, d).wait_recv()

    for c in range(2):
        pool[c, :per_row] = row[c][...]
        pool[c, per_row:] = inbox[c][...]
    starts = []
    for i in range(TOPN):
        j = sel[position, i]
        owner, rank = home(j)
        near = same(owner, b)
        entry = near * rank + (1 - near) * (per_row + owner)
        starts.append(j * SEL_BLOCK)
        for c, into in ((0, fk), (1, fv)):
            into[pl.ds(i * SEL_BLOCK, SEL_BLOCK), :] = pool[c, entry]
    fvt[...] = fv[...].T

    def fine_step(step, carry):
        start = pl.multiple_of(step * ROWS, ROWS)
        s = across(fk[...], query_block(start))
        k, q = iotas(SEL_BLOCK)
        ahead = k - q
        parts = [
            jnp.where(
                ahead <= first + start - starts[i], s[i * SEL_BLOCK : (i + 1) * SEL_BLOCK], NEG
            )
            for i in range(TOPN)
        ]
        s = jnp.concatenate(parts, axis=0)
        mixed, total = branch([s], [fvt[...]], False)
        mixed = acc[step] + mixed * (gate(1, start) / total)
        for h in range(HEADS):
            out[pl.ds(start, ROWS), h * HEAD_DIM : (h + 1) * HEAD_DIM] = mixed[
                :, h * ROWS : (h + 1) * ROWS
            ].T.astype(BF16)
        return carry

    lax.fori_loop(0, T // ROWS, fine_step, 0)

    for c in range(2):
        for e in range(1, Y):
            over_y(c, e).wait_send()
        for e in range(Y):
            to_mate(c, e).wait_send()

        @pl.when(last)
        def _(c=c):
            to_next(c).wait_send()

        for d in range(1, B):

            @pl.when(b + d < B)
            def _(c=c, d=d):
                block_out(c, d).wait_send()

    for d in range(1, B):

        @pl.when(b + d < B)
        def _(d=d):
            coarse_out(d).wait_send()

    for e in range(1, G):
        coarse_share(e).wait_send()


def per_device(
    queries, keys, values, selected, key_in, key_out, value_in, value_out, positions, gate_weight
):
    B = lax.axis_size("blk")
    G = lax.axis_size("grp")
    T = keys.shape[0]
    N = T // CMP_BLOCK
    Y = G // 2
    inner, hidden = key_in.shape
    vmem = pl.BlockSpec(memory_space=pltpu.VMEM)
    smem = pl.BlockSpec(memory_space=pltpu.SMEM)
    hbm = pl.BlockSpec(memory_space=pl.ANY)
    dma = pltpu.SemaphoreType.DMA

    def buf(*shape, dtype=BF16):
        return pltpu.VMEM(shape, dtype)

    return pl.pallas_call(
        functools.partial(kernel, B, G),
        out_shape=jax.ShapeDtypeStruct(queries.shape, BF16),
        in_specs=[smem, vmem, vmem, vmem, hbm, hbm, hbm, hbm, vmem, vmem],
        out_specs=vmem,
        scratch_shapes=[
            buf(2, inner, hidden),
            buf(2, hidden, HEAD_DIM),
            buf(2, T, HEAD_DIM, dtype=F32),
            buf(G * T // SEL_BLOCK, SEL_BLOCK, HEAD_DIM),
            buf(G * T // SEL_BLOCK, SEL_BLOCK, HEAD_DIM),
            buf(T // SEL_BLOCK, SEL_BLOCK, HEAD_DIM),
            buf(T // SEL_BLOCK, SEL_BLOCK, HEAD_DIM),
            buf(B, SEL_BLOCK, HEAD_DIM),
            buf(B, SEL_BLOCK, HEAD_DIM),
            buf(B - 1, SEL_BLOCK, HEAD_DIM),
            buf(B - 1, SEL_BLOCK, HEAD_DIM),
            buf(G, 2, B * N, HEAD_DIM),
            buf(HEAD_DIM, G * B * N),
            buf(2 * T, HEAD_DIM),
            buf(HEAD_DIM, 2 * T),
            buf(TOPN * SEL_BLOCK, HEAD_DIM),
            buf(TOPN * SEL_BLOCK, HEAD_DIM),
            buf(HEAD_DIM, TOPN * SEL_BLOCK),
            buf(2, G * T // SEL_BLOCK + B, SEL_BLOCK, HEAD_DIM),
            buf(T // ROWS, HEAD_DIM, HEADS * ROWS, dtype=F32),
            buf(3 * HEADS, T, dtype=F32),
            dma((4,)),
            dma((2, Y)),
            dma((2, Y)),
            dma((2, Y)),
            dma((2, Y)),
            dma((2,)),
            dma((2,)),
            dma((2, B)),
            dma((2, B)),
            dma((B,)),
            dma((B,)),
            dma((G,)),
            dma((G,)),
        ],
        compiler_params=pltpu.CompilerParams(
            collective_id=0, has_side_effects=True, vmem_limit_bytes=56 << 20
        ),
    )(
        selected,
        queries,
        keys.reshape(T // SEL_BLOCK, SEL_BLOCK, HEAD_DIM),
        values.reshape(T // SEL_BLOCK, SEL_BLOCK, HEAD_DIM),
        key_in,
        key_out,
        value_in,
        value_out,
        positions,
        gate_weight,
    )


def solution(mesh):
    rows = P(("blk", "grp"), None)
    return jax.shard_map(
        per_device,
        mesh=mesh,
        in_specs=(rows, rows, rows, P(), P(), P(), P(), P(), P(), P()),
        out_specs=rows,
        check_vma=False,
    )
```

```python
import functools
import math

import jax
import jax.numpy as jnp
from jax import lax
from jax.experimental import pallas as pl
from jax.experimental.pallas import tpu as pltpu
from jax.sharding import PartitionSpec as P

HEAD_DIM = 128
HEADS = 4
CMP_BLOCK = 32
SEL_BLOCK = 64
TOPN = 16
WINDOW = 512
ROWS = 128

NEG = -1e30
RATE = HEAD_DIM**-0.5 * math.log2(math.e)
MESH = pl.DeviceIdType.MESH
F32 = jnp.float32
BF16 = jnp.bfloat16


def across(a, b):
    return lax.dot_general(a, b, (((1,), (1,)), ((), ())), preferred_element_type=F32)


def branch(parts, value_parts, floor):
    top = functools.reduce(jnp.maximum, [jnp.max(s, axis=0, keepdims=True) for s in parts])
    total = 0.0
    if floor:
        top = jnp.maximum(top, 0.0)
        total = jnp.exp2(-top * RATE)
    mixed = 0.0
    for s, v in zip(parts, value_parts):
        weights = jnp.exp2((s - top) * RATE)
        total = total + jnp.sum(weights, axis=0, keepdims=True)
        mixed = mixed + jnp.dot(v, weights.astype(BF16), preferred_element_type=F32)
    return mixed, total


def kernel(
    B,
    G,
    sel,
    queries,
    keys,
    values,
    key_in,
    key_out,
    value_in,
    value_out,
    positions,
    gate_weight,
    out,
    w_in,
    w_out,
    shifted,
    sk,
    sv,
    pk,
    pv,
    ik,
    iv,
    stk,
    stv,
    cc,
    cvt,
    wk,
    wvt,
    fk,
    fv,
    fvt,
    ends,
    pool,
    acc,
    gates,
    w_sem,
    a_s,
    a_r,
    m_s,
    m_r,
    p_s,
    p_r,
    b_s,
    b_r,
    c_s,
    c_r,
    f_s,
    f_r,
):
    T = keys.shape[0] * SEL_BLOCK
    N = T // CMP_BLOCK
    Y = G // 2
    per_row = G * T // SEL_BLOCK
    b = lax.axis_index("blk")
    g = lax.axis_index("grp")
    y = g // 2
    core = g % 2
    mate = g + 1 - 2 * core
    position = b * G + g
    first = position * T

    loads = [
        pltpu.make_async_copy(src, dst, w_sem.at[n])
        for n, (src, dst) in enumerate(
            (
                (key_in, w_in.at[0]),
                (value_in, w_in.at[1]),
                (key_out, w_out.at[0]),
                (value_out, w_out.at[1]),
            )
        )
    ]
    for load in loads:
        load.start()

    cc[...] = jnp.zeros_like(cc)
    pk[...] = jnp.zeros_like(pk)
    pv[...] = jnp.zeros_like(pv)

    def remote(src, dst, send, recv, dev):
        return pltpu.make_async_remote_copy(
            src_ref=src,
            dst_ref=dst,
            send_sem=send,
            recv_sem=recv,
            device_id=dev,
            device_id_type=MESH,
        )

    def at(stretch, column):
        return {"blk": stretch, "grp": column}

    last = jnp.logical_and(g == 0, b < B - 1)
    head = jnp.logical_and(g == 0, b > 0)
    barrier = pltpu.get_barrier_semaphore()

    def greet(dev):
        pl.semaphore_signal(barrier, inc=1, device_id=dev, device_id_type=MESH)

    for e in range(1, G):
        greet(at(b, (g + e) % G))
    for d in range(1, B):
        greet(at((b + d) % B, g))

    here = pl.ds(g * (T // SEL_BLOCK), T // SEL_BLOCK)
    sk[here] = keys[...]
    sv[here] = values[...]
    def home(j):
        owner = lax.div(j, per_row)
        return owner, j - owner * per_row

    def same(left, right):
        gap = left - right
        return 1 - jnp.minimum(jnp.maximum(gap, -gap), 1)

    picks = []
    for d in range(1, B):
        line = jnp.minimum(b + d, B - 1) * G + g
        pick = jnp.int32(0)
        for i in range(TOPN):
            owner, rank = home(sel[i, line])
            pick = pick + same(owner, b) * rank
        picks.append(pick)

    gates[...] = jax.nn.sigmoid(
        lax.dot_general(
            gate_weight[...], queries[...], (((1,), (1,)), ((), ())), preferred_element_type=F32
        )
    )

    pl.semaphore_wait(barrier, G - 1 + B - 1)

    own = (keys, values)
    row = (sk, sv)
    prev = (pk, pv)
    staged = (stk, stv)
    inbox = (ik, iv)

    def slot(column):
        return pl.ds(column * (T // SEL_BLOCK), T // SEL_BLOCK)

    def over_y(c, e):
        return remote(
            own[c], row[c].at[slot(g)], a_s.at[c, e], a_r.at[c, e], at(b, ((y + e) % Y) * 2 + core)
        )

    def to_mate(c, e):
        source = ((y - e + Y) % Y) * 2 + core
        src = own[c] if e == 0 else row[c].at[slot(source)]
        return remote(src, row[c].at[slot(source)], m_s.at[c, e], m_r.at[c, e], at(b, mate))

    def to_next(c):
        return remote(
            row[c].at[slot(G - 1)], prev[c], p_s.at[c], p_r.at[c], at((b + 1) % B, 0)
        )

    def block_out(c, d):
        return remote(
            staged[c].at[d - 1], inbox[c].at[b], b_s.at[c, d], b_r.at[c, d], at((b + d) % B, g)
        )

    def coarse_out(d):
        part = cc.at[g, :, pl.ds(pl.multiple_of(b * N, N), N), :]
        return remote(part, part, c_s.at[d], c_r.at[d], at((b + d) % B, g))

    def coarse_over_y(e):
        return remote(
            cc.at[g], cc.at[g], f_s.at[0, e], f_r.at[0, e], at(b, ((y + e) % Y) * 2 + core)
        )

    def coarse_to_mate(e):
        part = cc.at[((y - e + Y) % Y) * 2 + core]
        return remote(part, part, f_s.at[1, e], f_r.at[1, e], at(b, mate))

    for c in range(2):
        for e in range(1, Y):
            over_y(c, e).start()
        to_mate(c, 0).start()

    for c in range(2):
        shift = positions[c].astype(F32)
        shifted[c] = (
            own[c][...].astype(F32).reshape(N, CMP_BLOCK, HEAD_DIM) + shift[None]
        ).reshape(T, HEAD_DIM)
    for load in loads:
        load.wait()
    mine_rows = pl.ds(pl.multiple_of(b * N, N), N)
    for c in range(2):
        flat = jnp.concatenate(
            [shifted[c, pl.ds(t, N, stride=CMP_BLOCK), :].astype(BF16) for t in range(CMP_BLOCK)],
            axis=1,
        )
        hidden = jax.nn.silu(jnp.dot(flat, w_in[c], preferred_element_type=F32)).astype(BF16)
        cc[g, c, mine_rows, :] = jnp.dot(hidden, w_out[c], preferred_element_type=F32).astype(BF16)
    for d in range(1, B):

        @pl.when(b + d < B)
        def _(d=d):
            coarse_out(d).start()

    for e in range(1, Y):
        over_y(0, e).wait_recv()
        to_mate(0, e).start()
    for d in range(1, B):

        @pl.when(b - d >= 0)
        def _(d=d):
            coarse_out(d).wait_recv()

    for e in range(1, Y):
        coarse_over_y(e).start()
    coarse_to_mate(0).start()

    for c in range(2):
        if c == 1:
            for e in range(1, Y):
                over_y(c, e).wait_recv()
                to_mate(c, e).start()
        for e in range(Y):
            to_mate(c, e).wait_recv()
        for d in range(1, B):

            @pl.when(b + d < B)
            def _(c=c, d=d):
                staged[c][d - 1] = row[c][picks[d - 1]]

        for d in range(1, B):

            @pl.when(b + d < B)
            def _(c=c, d=d):
                block_out(c, d).start()

        @pl.when(last)
        def _(c=c):
            to_next(c).start()

    for e in range(1, Y):
        coarse_over_y(e).wait_recv()
        coarse_to_mate(e).start()

    lanes = HEADS * ROWS

    def query_block(start):
        rows = queries[pl.ds(start, ROWS), :]
        return jnp.concatenate(
            [rows[:, h * HEAD_DIM : (h + 1) * HEAD_DIM] for h in range(HEADS)], axis=0
        )

    def gate(n, start):
        return jnp.concatenate(
            [gates[n * HEADS + h : n * HEADS + h + 1, pl.ds(start, ROWS)] for h in range(HEADS)],
            axis=1,
        )

    def iotas(count):
        k = lax.broadcasted_iota(jnp.int32, (count, lanes), 0)
        q = lax.broadcasted_iota(jnp.int32, (count, lanes), 1) % ROWS
        return k, q

    for e in range(Y):
        coarse_to_mate(e).wait_recv()
    for column in range(G):
        cvt[:, pl.ds(column * B * N, B * N)] = cc[column, 1].T

    k, q = iotas(B * N)
    ends[...] = (k // N) * (G * T) + (k % N) * CMP_BLOCK + CMP_BLOCK - 1 - q

    def coarse_step(step, carry):
        start = pl.multiple_of(step * ROWS, ROWS)
        query = query_block(start)
        parts = []
        for column in range(G):
            s = across(cc[column, 0], query)
            parts.append(jnp.where(ends[...] <= first + start - column * T, s, NEG))
        vts = [cvt[:, pl.ds(column * B * N, B * N)] for column in range(G)]
        mixed, total = branch(parts, vts, True)
        acc[step] = mixed * (gate(0, start) / total)
        return carry

    lax.fori_loop(0, T // ROWS, coarse_step, 0, unroll=True)

    @pl.when(head)
    def _():
        for c in range(2):
            to_next(c).wait_recv()

    before = slot(jnp.maximum(g - 1, 0))
    flat = (T, HEAD_DIM)
    wk[pl.ds(0, T), :] = jnp.where(g == 0, pk[...], sk[before]).reshape(flat)
    wk[pl.ds(T, T), :] = keys[...].reshape(flat)
    wvt[:, pl.ds(0, T)] = jnp.where(g == 0, pv[...], sv[before]).reshape(flat).T
    wvt[:, pl.ds(T, T)] = values[...].reshape(flat).T

    def window_step(step, carry):
        start = pl.multiple_of(step * ROWS, ROWS)
        span = pl.ds(pl.multiple_of(start + T - WINDOW, ROWS), ROWS + WINDOW)
        s = across(wk[span, :], query_block(start))
        k, q = iotas(ROWS)
        opening = jnp.where(position == 0, WINDOW - start, 0)
        kk = lax.broadcasted_iota(jnp.int32, (WINDOW - ROWS, lanes), 0) + ROWS
        parts = [
            jnp.where((k > q) & (k >= opening), s[:ROWS], NEG),
            jnp.where(kk >= opening, s[ROWS:WINDOW], NEG),
            jnp.where(k <= q, s[WINDOW:], NEG),
        ]
        vt = wvt[:, span]
        mixed, total = branch(parts, [vt[:, :ROWS], vt[:, ROWS:WINDOW], vt[:, WINDOW:]], False)
        acc[step] = acc[step] + mixed * (gate(2, start) / total)
        return carry

    lax.fori_loop(0, T // ROWS, window_step, 0, unroll=True)

    for c in range(2):
        for d in range(1, B):

            @pl.when(b - d >= 0)
            def _(c=c, d=d):
                block_out(c, d).wait_recv()

    for c in range(2):
        pool[c, :per_row] = row[c][...]
        pool[c, per_row:] = inbox[c][...]
    starts = []
    for i in range(TOPN):
        j = sel[i, position]
        owner, rank = home(j)
        near = same(owner, b)
        entry = near * rank + (1 - near) * (per_row + owner)
        starts.append(j * SEL_BLOCK)
        for c, into in ((0, fk), (1, fv)):
            into[pl.ds(i * SEL_BLOCK, SEL_BLOCK), :] = pool[c, entry]
    fvt[...] = fv[...].T

    def fine_step(step, carry):
        start = pl.multiple_of(step * ROWS, ROWS)
        s = across(fk[...], query_block(start))
        k, q = iotas(SEL_BLOCK)
        ahead = k - q
        parts = [
            jnp.where(
                ahead <= first + start - starts[i], s[i * SEL_BLOCK : (i + 1) * SEL_BLOCK], NEG
            )
            for i in range(TOPN)
        ]
        s = jnp.concatenate(parts, axis=0)
        mixed, total = branch([s], [fvt[...]], False)
        mixed = acc[step] + mixed * (gate(1, start) / total)
        for h in range(HEADS):
            out[pl.ds(start, ROWS), h * HEAD_DIM : (h + 1) * HEAD_DIM] = mixed[
                :, h * ROWS : (h + 1) * ROWS
            ].T.astype(BF16)
        return carry

    lax.fori_loop(0, T // ROWS, fine_step, 0, unroll=True)

    for c in range(2):
        for e in range(1, Y):
            over_y(c, e).wait_send()
        for e in range(Y):
            to_mate(c, e).wait_send()

        @pl.when(last)
        def _(c=c):
            to_next(c).wait_send()

        for d in range(1, B):

            @pl.when(b + d < B)
            def _(c=c, d=d):
                block_out(c, d).wait_send()

    for d in range(1, B):

        @pl.when(b + d < B)
        def _(d=d):
            coarse_out(d).wait_send()

    for e in range(1, Y):
        coarse_over_y(e).wait_send()
    for e in range(Y):
        coarse_to_mate(e).wait_send()


def per_device(
    queries, keys, values, selected, key_in, key_out, value_in, value_out, positions, gate_weight
):
    B = lax.axis_size("blk")
    G = lax.axis_size("grp")
    T = keys.shape[0]
    N = T // CMP_BLOCK
    Y = G // 2
    inner, hidden = key_in.shape
    vmem = pl.BlockSpec(memory_space=pltpu.VMEM)
    smem = pl.BlockSpec(memory_space=pltpu.SMEM)
    hbm = pl.BlockSpec(memory_space=pl.ANY)
    dma = pltpu.SemaphoreType.DMA

    def buf(*shape, dtype=BF16):
        return pltpu.VMEM(shape, dtype)

    return pl.pallas_call(
        functools.partial(kernel, B, G),
        out_shape=jax.ShapeDtypeStruct(queries.shape, BF16),
        in_specs=[smem, vmem, vmem, vmem, hbm, hbm, hbm, hbm, vmem, vmem],
        out_specs=vmem,
        scratch_shapes=[
            buf(2, inner, hidden),
            buf(2, hidden, HEAD_DIM),
            buf(2, T, HEAD_DIM, dtype=F32),
            buf(G * T // SEL_BLOCK, SEL_BLOCK, HEAD_DIM),
            buf(G * T // SEL_BLOCK, SEL_BLOCK, HEAD_DIM),
            buf(T // SEL_BLOCK, SEL_BLOCK, HEAD_DIM),
            buf(T // SEL_BLOCK, SEL_BLOCK, HEAD_DIM),
            buf(B, SEL_BLOCK, HEAD_DIM),
            buf(B, SEL_BLOCK, HEAD_DIM),
            buf(B - 1, SEL_BLOCK, HEAD_DIM),
            buf(B - 1, SEL_BLOCK, HEAD_DIM),
            buf(G, 2, B * N, HEAD_DIM),
            buf(HEAD_DIM, G * B * N),
            buf(2 * T, HEAD_DIM),
            buf(HEAD_DIM, 2 * T),
            buf(TOPN * SEL_BLOCK, HEAD_DIM),
            buf(TOPN * SEL_BLOCK, HEAD_DIM),
            buf(HEAD_DIM, TOPN * SEL_BLOCK),
            buf(B * N, HEADS * ROWS, dtype=jnp.int32),
            buf(2, G * T // SEL_BLOCK + B, SEL_BLOCK, HEAD_DIM),
            buf(T // ROWS, HEAD_DIM, HEADS * ROWS, dtype=F32),
            buf(3 * HEADS, T, dtype=F32),
            dma((4,)),
            dma((2, Y)),
            dma((2, Y)),
            dma((2, Y)),
            dma((2, Y)),
            dma((2,)),
            dma((2,)),
            dma((2, B)),
            dma((2, B)),
            dma((B,)),
            dma((B,)),
            dma((2, Y)),
            dma((2, Y)),
        ],
        compiler_params=pltpu.CompilerParams(
            collective_id=0, has_side_effects=True, vmem_limit_bytes=56 << 20
        ),
    )(
        selected.T,
        queries,
        keys.reshape(T // SEL_BLOCK, SEL_BLOCK, HEAD_DIM),
        values.reshape(T // SEL_BLOCK, SEL_BLOCK, HEAD_DIM),
        key_in,
        key_out,
        value_in,
        value_out,
        positions,
        gate_weight.T,
    )


def solution(mesh):
    rows = P(("blk", "grp"), None)
    return jax.shard_map(
        per_device,
        mesh=mesh,
        in_specs=(rows, rows, rows, P(), P(), P(), P(), P(), P(), P()),
        out_specs=rows,
        check_vma=False,
    )
```
